32 devices in a mesh: lat: 4 (over z), lon: 8 (over y, x, core).
Axes of the slice: x: 2, y: 2, z: 4, core: 2. Of those that a mesh axis runs over, the one named last changes fastest.
Arguments:
- background: bfloat16 [32768, 384], P(('lat', 'lon')), may hold values from -6 to 6
- increment: bfloat16 [32768, 384], P(('lat', 'lon')), may hold values from -6 to 6
- coefficients: bfloat16 [384, 4352], replicated, may hold values from -0.3125 to 0.3125
- departures: bfloat16 [128, 128, 4352], P(('lat', 'lon')), may hold values from -6 to 6
- bias_pred: float32 [128, 128, 8], P(('lat', 'lon')), may hold values from -6 to 6
- beta_incr: float32 [8, 4352], replicated, may hold values from -2 to 2
- obs_weight: float32 [4352], replicated, may hold values from 0.1 to 1
- obs_count: int32 [128], P(('lat', 'lon')), may hold values from 1 to 128
- col_index: int32 [128, 128], P(('lat', 'lon')), may hold values from 0 to 32767, as said below
Outputs:
- radiance: bfloat16 [128, 128, 4352], P(('lat', 'lon'))
- column_grad: bfloat16 [32768, 384], P(('lat', 'lon'))
- bias_grad: float32 [4352, 8], P(('lat', 'lon'))
The draws below stay inside these ranges and needn't reach their ends.
Inputs may be any that keep to these rules, and one draw needn't show every extreme that they name: `col_index`: column c is owned by the block of 1024 columns c // 1024. Among the 512 slots of the blocks of one device, at most 24 name columns of any one owner, and some owner is named by exactly 24 slots of every device.
All inputs are finite; a program needn't handle non-finite values.
Results may differ from the reference program's by a relative error of at most 0.005.
Values may be sent and summed in bfloat16 or wider, within the bound.
A program may use at most 128 MiB of HBM per device.

```python
import math
import jax
import jax.numpy as jnp
from jax import lax

P_SIZE = 384
CH = 4352
NPRED = 8
COLS_DEV = 1024
BLK = 128
NB_DEV = 4
NCOLS = 32768
NBLOCKS = 128
N_LAT = 4
N_LON = 8


def draw_col_index(key, part):
    devices = N_LAT * N_LON
    slot_count = NB_DEV * BLK
    quota = slot_count // (2 * devices)
    common_owner = jax.random.randint(jax.random.fold_in(key, 7), (), 0, devices).astype(jnp.int32)

    def one_device(device_index):
        device_key = jax.random.fold_in(key, device_index + 11)
        key_perm, key_order, key_local = jax.random.split(device_key, 3)
        others = (common_owner + 1 + jax.random.permutation(key_perm, devices - 1).astype(jnp.int32)) % devices
        hot_owners = jnp.concatenate([common_owner[None], others[:devices // 2 - 1]])
        spread_owners = jnp.arange(devices * quota, dtype=jnp.int32) // quota
        hot_extra = jnp.repeat(hot_owners, 2 * quota, total_repeat_length=devices * quota).astype(jnp.int32)
        owners = jnp.concatenate([spread_owners, hot_extra])
        owners = jax.random.permutation(key_order, owners).astype(jnp.int32)
        local_cols = jax.random.randint(key_local, (slot_count,), 0, COLS_DEV).astype(jnp.int32)
        return owners * COLS_DEV + local_cols
    columns = jax.vmap(one_device)(jnp.arange(devices, dtype=jnp.int32))
    return columns.reshape(NB_DEV * devices, BLK).astype(jnp.int32)


def touch_ends(result, own_key, low, largest):
    longest = result.shape.index(max(result.shape))
    spots = []
    for shift in (0, 1):
        where = [jax.random.randint(jax.random.fold_in(own_key, axis), (), 0, length) for axis, length in enumerate(result.shape)]
        where[longest] = (where[longest] + shift) % result.shape[longest]
        spots.append(tuple(where))
    return result.at[spots[0]].set(low).at[spots[1]].set(largest)


def spiked(drawn, stream_key, source, target, parts, factor):
    owner, partner = [(jnp.arange(drawn.shape[dim]) // (drawn.shape[dim] // parts)).reshape([-1 if axis == dim else 1 for axis in range(drawn.ndim)]) for dim in (source, target)]
    chosen = jax.random.permutation(stream_key, parts)[partner]
    strong = (owner == chosen) | (owner == (partner + parts // 2) % parts)
    return jnp.where(strong, factor * drawn, drawn)


def block_levels(stream_key, dims, shards, smallest, top_value):
    loudness, own = 1.0, jax.random.fold_in(stream_key, 6)
    for position, blocks in shards:
        heights = jnp.exp(jax.random.uniform(jax.random.fold_in(own, position), (blocks,), jnp.float32, smallest / len(shards), top_value / len(shards)))
        loudness = loudness * jnp.repeat(heights, dims[position] // blocks).reshape([-1 if axis == position else 1 for axis in range(len(dims))])
    return loudness


def bell_draw(rng, dims, width, bound, cuts=(), held_as=jnp.bfloat16):
    factor_of = block_levels(rng, dims, cuts, -0.22, 0.18) if cuts else 1.0
    values = jax.random.normal(rng, dims, jnp.float32) * width * factor_of
    return jnp.minimum(jnp.maximum(values, -bound), bound).astype(held_as)


def bell_draw_with(stream_key, dims, width, limit, shards, heavy, kind=jnp.bfloat16):
    drawn = width * jax.random.normal(stream_key, dims, jnp.float32)
    if shards:
        drawn = drawn * block_levels(stream_key, dims, shards, -0.22, 0.18)
    return jnp.clip(spiked(drawn, jax.random.fold_in(stream_key, 3), *heavy), -limit, limit).astype(kind)


def setup_inputs(seed: int = 0) -> dict:
    key_list = jax.random.split(jax.random.key(seed), 10)
    background = bell_draw(key_list[0], (NCOLS, P_SIZE), 1.0, 6.0, ((0, 32),))
    increment = bell_draw(key_list[1], (NCOLS, P_SIZE), 1.0, 6.0, ((0, 32),))
    coefficients = bell_draw(key_list[2], (P_SIZE, CH), P_SIZE ** -0.5, 0.3125)
    departures = bell_draw_with(key_list[3], (NBLOCKS, BLK, CH), 1.0, 6.0, ((0, 32),), (0, 2, 32, 2.75))
    bias_pred = bell_draw(key_list[4], (NBLOCKS, BLK, NPRED), 1.0, 6.0, ((0, 32),), jnp.float32)
    beta_incr = bell_draw(key_list[5], (NPRED, CH), NPRED ** -0.5, 2.0, (), jnp.float32)
    obs_weight = jnp.clip(jnp.exp(jax.random.uniform(key_list[6], (CH,), jnp.float32, math.log(0.1), math.log(1.0))), 0.1, 1.0)
    obs_count = touch_ends(jax.random.randint(key_list[7], (NBLOCKS,), 1, BLK + 1), jax.random.fold_in(key_list[7], 1), 1, BLK).astype(jnp.int32)
    col_index = draw_col_index(jax.random.fold_in(key_list[9], 71), 0)
    return {"background": background, "increment": increment, "coefficients": coefficients, "departures": departures, "bias_pred": bias_pred, "beta_incr": beta_incr, "obs_weight": obs_weight, "obs_count": obs_count, "col_index": col_index}


def reference(background, increment, coefficients, departures, bias_pred, beta_incr, obs_weight, obs_count, col_index):
    devices = N_LAT * N_LON
    slot_count = NB_DEV * BLK
    scaling = 1.0 / jnp.sqrt(jnp.float32(NBLOCKS * BLK))
    grouped_cols = col_index.reshape(devices, slot_count)
    grouped_deps = departures.reshape(devices, slot_count, CH)
    grouped_pred = bias_pred.reshape(devices, slot_count, NPRED)
    grouped_counts = obs_count.reshape(devices, NB_DEV)

    def accumulate(gradient, group):
        columns, misfits_in, predictors_in, counts = group
        slot_pos = jnp.arange(BLK, dtype=jnp.int32)
        present = (slot_pos[None, :] < counts[:, None]).reshape(slot_count, 1)
        base_rows = background[columns]
        step_rows = increment[columns]
        jacobian = 1.0 + 0.5 * jnp.tanh(base_rows.astype(jnp.float32))
        predictor = (step_rows.astype(jnp.float32) * jacobian).astype(jnp.bfloat16)
        radiance_f = jnp.dot(predictor, coefficients, preferred_element_type=jnp.float32)
        radiance_f = radiance_f + jnp.dot(predictors_in, beta_incr, precision=lax.Precision.HIGHEST)
        radiance_f = jnp.where(present, radiance_f, jnp.float32(0.0))
        misfit = jnp.where(present, obs_weight[None, :] * (radiance_f - misfits_in.astype(jnp.float32)), jnp.float32(0.0))
        pulled = jnp.dot(misfit.astype(jnp.bfloat16), coefficients.T, preferred_element_type=jnp.float32)
        gradient = gradient.at[columns].add(pulled * jacobian)
        bias_part = jnp.dot(misfit.T, predictors_in, precision=lax.Precision.HIGHEST) * scaling
        return (gradient, (radiance_f.astype(jnp.bfloat16), bias_part))
    start = jnp.zeros((NCOLS, P_SIZE), jnp.float32)
    gradient, (radiances, bias_parts) = lax.scan(accumulate, start, (grouped_cols, grouped_deps, grouped_pred, grouped_counts))
    return (radiances.reshape(NBLOCKS, BLK, CH), gradient.astype(jnp.bfloat16), lax.optimization_barrier(jnp.sum(bias_parts, axis=0)))
```

```python
import jax
import jax.numpy as jnp
from jax import lax
from jax.sharding import PartitionSpec as P


def route_ids(requests):
    return lax.all_to_all(requests, ("lat", "lon"), split_axis=0, concat_axis=0, tiled=True)


def route_profiles(payload):
    return lax.all_to_all(payload, ("lat", "lon"), split_axis=0, concat_axis=0, tiled=True)


def route_adjoint(payload):
    return lax.all_to_all(payload, ("lat", "lon"), split_axis=0, concat_axis=0, tiled=True)


def shards(
    background,
    increment,
    coefficients,
    departures,
    bias_pred,
    beta_incr,
    obs_weight,
    obs_count,
    col_index,
):
    lat_count = lax.axis_size("lat")
    lon_count = lax.axis_size("lon")
    devices = lat_count * lon_count
    column_count, profile_len = background.shape
    block_count, block_len = col_index.shape
    channels = coefficients.shape[1]
    npredictors = bias_pred.shape[2]
    slot_count = block_count * block_len
    capacity = 3 * slot_count // (2 * devices)
    scaling = 1.0 / jnp.sqrt(jnp.float32(slot_count * devices))
    columns = col_index.reshape(slot_count)
    owners = columns // column_count
    local_cols = columns % column_count
    owner_table = (owners[:, None] == jnp.arange(devices, dtype=jnp.int32)[None, :]).astype(
        jnp.int32
    )
    bucket_rank = jnp.sum(jnp.cumsum(owner_table, axis=0) * owner_table, axis=1) - 1
    position = owners * capacity + bucket_rank
    requests = jnp.zeros((devices * capacity,), jnp.int32).at[position].set(local_cols)
    wanted = route_ids(requests.reshape(devices, capacity)).reshape(devices * capacity)
    base_rows = background[wanted]
    step_rows = increment[wanted]
    owner_jacobian = 1.0 + 0.5 * jnp.tanh(base_rows.astype(jnp.float32))
    formed_rows = (step_rows.astype(jnp.float32) * owner_jacobian).astype(jnp.bfloat16)
    arrived = route_profiles(formed_rows.reshape(devices, capacity, profile_len))
    predictor = arrived.reshape(devices * capacity, profile_len)[position]
    flat_pred = bias_pred.reshape(slot_count, npredictors)
    slot_pos = jnp.arange(block_len, dtype=jnp.int32)
    present = (slot_pos[None, :] < obs_count[:, None]).reshape(slot_count, 1)
    radiance_f = jnp.dot(predictor, coefficients, preferred_element_type=jnp.float32)
    radiance_f = radiance_f + jnp.dot(flat_pred, beta_incr, precision=lax.Precision.HIGHEST)
    radiance_f = jnp.where(present, radiance_f, jnp.float32(0.0))
    radiance = radiance_f.astype(jnp.bfloat16).reshape(block_count, block_len, channels)
    observed = departures.reshape(slot_count, channels).astype(jnp.float32)
    misfit = jnp.where(present, obs_weight[None, :] * (radiance_f - observed), jnp.float32(0.0))
    pulled = lax.dot_general(
        misfit.astype(jnp.bfloat16),
        coefficients,
        (((1,), (1,)), ((), ())),
        preferred_element_type=jnp.float32,
    )
    outgoing = jnp.zeros((devices * capacity, profile_len), jnp.bfloat16).at[position].set(
        pulled.astype(jnp.bfloat16)
    )
    returned = route_adjoint(outgoing.reshape(devices, capacity, profile_len))
    returned = returned.reshape(devices * capacity, profile_len).astype(jnp.float32) * owner_jacobian
    gradient = jnp.zeros((column_count, profile_len), jnp.float32).at[wanted].add(returned)
    column_grad = gradient.astype(jnp.bfloat16)
    local_bias = (
        lax.dot_general(
            flat_pred, misfit, (((0,), (0,)), ((), ())), precision=lax.Precision.HIGHEST
        )
        * scaling
    )
    pieces = local_bias.reshape(npredictors, devices, channels // devices).transpose(1, 0, 2)
    shares = lax.all_to_all(pieces, ("lat", "lon"), split_axis=0, concat_axis=0, tiled=True)
    bias_grad = jnp.sum(shares, axis=0).T
    return (radiance, column_grad, bias_grad)


def solution(mesh):
    return jax.shard_map(
        shards,
        mesh=mesh,
        in_specs=(
            P(("lat", "lon"), None),
            P(("lat", "lon"), None),
            P(),
            P(("lat", "lon"), None, None),
            P(("lat", "lon"), None, None),
            P(),
            P(),
            P(("lat", "lon")),
            P(("lat", "lon"), None),
        ),
        out_specs=(P(("lat", "lon"), None, None), P(("lat", "lon"), None), P(("lat", "lon"), None)),
        check_vma=False,
    )
```

```python
import functools

import jax
import jax.numpy as jnp
from jax import lax
from jax.experimental import pallas as pl
from jax.experimental.pallas import tpu as pltpu
from jax.sharding import PartitionSpec as P

MESH = pl.DeviceIdType.MESH
VMEM = pl.BlockSpec(memory_space=pltpu.VMEM)
SPAN = 128
GRANT = 60 * 1024 * 1024


def peers_of(lat_count, lon_count):
    devices = lat_count * lon_count
    me = lax.axis_index("lat") * lon_count + lax.axis_index("lon")

    def peer(offset):
        other = lax.rem(me + offset, devices)
        return other, (lax.div(other, lon_count), lax.rem(other, lon_count))

    return me, peer


def greet(devices, peer):
    barrier = pltpu.get_barrier_semaphore()

    def one(offset, carry):
        pl.semaphore_signal(barrier, inc=1, device_id=peer(offset)[1], device_id_type=MESH)
        return carry

    lax.fori_loop(1, devices, one, 0)
    return barrier


def send_all(devices, me, peer, source, target, send_sem, recv_sem):
    def one(offset, carry):
        other, where = peer(offset)
        pltpu.make_async_remote_copy(
            src_ref=source.at[other],
            dst_ref=target.at[me],
            send_sem=send_sem.at[offset],
            recv_sem=recv_sem.at[me],
            device_id=where,
            device_id_type=MESH,
        ).start()
        return carry

    lax.fori_loop(1, devices, one, 0)


def wait_all(devices, peer, source, target, send_sem, recv_sem):
    def one(offset, carry):
        other, where = peer(offset)
        copy = pltpu.make_async_remote_copy(
            src_ref=source.at[other],
            dst_ref=target.at[other],
            send_sem=send_sem.at[offset],
            recv_sem=recv_sem.at[other],
            device_id=where,
            device_id_type=MESH,
        )
        copy.wait_recv()
        copy.wait_send()
        return carry

    lax.fori_loop(1, devices, one, 0)


def iota(shape, dim):
    return lax.broadcasted_iota(jnp.int32, shape, dim)


def ones_where(mask):
    return jnp.where(mask, jnp.float32(1.0), jnp.float32(0.0)).astype(jnp.bfloat16)


def dot(a, b):
    return jnp.dot(a, b, preferred_element_type=jnp.float32)


def dot_nt(a, b):
    return lax.dot_general(a, b, (((1,), (1,)), ((), ())), preferred_element_type=jnp.float32)


def fetch_kernel(
    lat_count,
    lon_count,
    capacity,
    cols_ref,
    base_ref,
    step_ref,
    pred_ref,
    position_ref,
    wanted_ref,
    ask,
    asked,
    formed,
    outbound,
    inbound,
    picker,
    ask_send,
    ask_recv,
    row_send,
    row_recv,
):
    devices = lat_count * lon_count
    column_count, profile_len = base_ref.shape
    slots = cols_ref.shape[1]
    rows = devices * capacity
    shift = column_count.bit_length() - 1
    assert column_count == 1 << shift
    me, peer = peers_of(lat_count, lon_count)
    barrier = greet(devices, peer)

    cols = cols_ref[...]
    owners = lax.shift_right_logical(cols, shift)
    local = cols & (column_count - 1)
    owned = jnp.where(iota((devices, slots), 0) == owners, jnp.float32(1.0), jnp.float32(0.0))
    before = ones_where(iota((slots, slots), 0) < iota((slots, slots), 1))
    ranks = dot(owned.astype(jnp.bfloat16), before)
    rank = jnp.sum(owned * ranks, axis=0, keepdims=True).astype(jnp.int32)
    position = owners * capacity + rank
    position_ref[...] = position
    spot = ones_where(iota((SPAN, slots), 0) == rank)
    high = lax.shift_right_logical(local, 8).astype(jnp.float32)
    low = (local & 255).astype(jnp.float32)
    asks = dot_nt((owned * high).astype(jnp.bfloat16), spot) * 256.0
    asks = asks + dot_nt((owned * low).astype(jnp.bfloat16), spot)
    ask[:, 0, :] = asks

    pl.semaphore_wait(barrier, devices - 1)
    send_all(devices, me, peer, ask, asked, ask_send, ask_recv)
    asked[me] = ask[me]
    jacobian = 1.0 + 0.5 * jnp.tanh(base_ref[...].astype(jnp.float32))
    formed[...] = (step_ref[...].astype(jnp.float32) * jacobian).astype(jnp.bfloat16)
    wait_all(devices, peer, ask, asked, ask_send, ask_recv)

    table = asked[:, 0, :].astype(jnp.int32)
    first = iota((rows, devices), 1) * capacity
    row = iota((rows, devices), 0)
    spread = ones_where((row >= first) & (row < first + capacity))
    table_high = lax.shift_right_logical(table, 8).astype(jnp.float32).astype(jnp.bfloat16)
    table_low = (table & 255).astype(jnp.float32).astype(jnp.bfloat16)
    listed = dot(spread, table_high) * 256.0 + dot(spread, table_low)
    row_f = iota((rows, SPAN), 0).astype(jnp.float32)
    within = row_f - capacity * jnp.floor((row_f + 0.5) * (1.0 / capacity))
    lane_f = iota((rows, SPAN), 1).astype(jnp.float32)
    wanted = jnp.sum(jnp.where(lane_f == within, listed, 0.0), axis=1, keepdims=True)
    wanted = wanted.astype(jnp.int32)
    chosen = ones_where(wanted == iota((rows, column_count), 1))
    payload = dot(chosen, formed[...]).reshape(devices, capacity, profile_len)
    outbound[...] = payload.astype(jnp.bfloat16)
    send_all(devices, me, peer, outbound, inbound, row_send, row_recv)
    inbound[me] = outbound[me]

    diagonal = iota((rows, rows), 0) == iota((rows, rows), 1)
    wanted_f = wanted.astype(jnp.float32)
    wanted_ref[...] = jnp.sum(
        jnp.where(diagonal, wanted_f, 0.0), axis=0, keepdims=True
    ).astype(jnp.int32)
    diagonal = iota((slots, slots), 0) == iota((slots, slots), 1)
    upright = jnp.sum(
        jnp.where(diagonal, position.astype(jnp.float32), 0.0), axis=1, keepdims=True
    ).astype(jnp.int32)
    picker[...] = ones_where(upright == iota((slots, rows), 1))
    wait_all(devices, peer, outbound, inbound, row_send, row_recv)
    arrived = inbound[...].astype(jnp.float32).reshape(rows, profile_len).astype(jnp.bfloat16)
    pred_ref[...] = dot(picker[...], arrived).astype(jnp.bfloat16)


def fetch(lat_count, lon_count, capacity, cols, background, increment):
    devices = lat_count * lon_count
    column_count, profile_len = background.shape
    slots = cols.shape[1]
    rows = devices * capacity
    return pl.pallas_call(
        functools.partial(fetch_kernel, lat_count, lon_count, capacity),
        out_shape=(
            jax.ShapeDtypeStruct((slots, profile_len), jnp.bfloat16),
            jax.ShapeDtypeStruct((1, slots), jnp.int32),
            jax.ShapeDtypeStruct((1, rows), jnp.int32),
        ),
        in_specs=[VMEM] * 3,
        out_specs=(VMEM,) * 3,
        scratch_shapes=[
            pltpu.VMEM((devices, 1, SPAN), jnp.float32),
            pltpu.VMEM((devices, 1, SPAN), jnp.float32),
            pltpu.VMEM((column_count, profile_len), jnp.bfloat16),
            pltpu.VMEM((devices, capacity, profile_len), jnp.bfloat16),
            pltpu.VMEM((devices, capacity, profile_len), jnp.bfloat16),
            pltpu.VMEM((slots, rows), jnp.bfloat16),
        ]
        + [pltpu.SemaphoreType.DMA((devices,))] * 4,
        compiler_params=pltpu.CompilerParams(
            collective_id=0, has_side_effects=True, vmem_limit_bytes=GRANT
        ),
        name="fetch_profiles",
    )(cols, background, increment)


def compute_kernel(
    block_len,
    scaling,
    count_ref,
    pred_ref,
    aug_ref,
    flip_ref,
    coef_ref,
    dep_ref,
    beta_ref,
    weight_ref,
    rad_ref,
    pulled_ref,
    bias_ref,
    left,
    total,
    main,
    rest,
):
    step = pl.program_id(0)
    profile_len = pred_ref.shape[1]
    npredictors, tile = beta_ref.shape

    @pl.when(step == 0)
    def _():
        left[:, :profile_len] = pred_ref[...]
        left[:, profile_len:] = aug_ref[...]
        total[...] = jnp.zeros_like(total)

    coef = coef_ref[...]
    beta = beta_ref[...]
    beta_main = beta.astype(jnp.bfloat16).astype(jnp.float32)
    beta_rest = beta - beta_main
    filler = jnp.zeros((SPAN - 3 * npredictors, tile), jnp.float32)
    extra = jnp.concatenate([beta_main, beta_rest, beta_main, filler], axis=0)
    right = jnp.concatenate([coef, extra.astype(jnp.bfloat16)], axis=0)
    weight = weight_ref[...]
    for block in range(pred_ref.shape[0] // block_len):
        part = pl.ds(block * block_len, block_len)
        present = iota((block_len, tile), 0) < count_ref[block]
        radiance = jnp.where(present, dot(left[part, :], right), 0.0)
        rad_ref[part, :] = radiance.astype(jnp.bfloat16)
        misfit = weight * (radiance - dep_ref[part, :].astype(jnp.float32))
        misfit = jnp.where(present, misfit, 0.0)
        misfit_b = misfit.astype(jnp.bfloat16)
        main[part, :] = misfit_b
        rest[part, :] = (misfit - misfit_b.astype(jnp.float32)).astype(jnp.bfloat16)
    total[...] += dot_nt(main[...], coef)
    whole = dot(flip_ref[...], main[...])
    small = dot(flip_ref[...], rest[...])
    bias_ref[...] = scaling * (
        whole[:npredictors] + whole[npredictors:] + small[:npredictors]
    )

    @pl.when(step == pl.num_programs(0) - 1)
    def _():
        pulled_ref[...] = total[...].astype(jnp.bfloat16)


def compute(block_len, scaling, obs_count, pred, flat_pred, coef, dep, beta, weight):
    slots, profile_len = pred.shape
    channels = coef.shape[1]
    npredictors = flat_pred.shape[1]
    tile = max(t for t in range(128, 513, 128) if channels % t == 0)
    main = lax.reduce_precision(flat_pred, 8, 7)
    rest = (flat_pred - main).astype(jnp.bfloat16)
    main = main.astype(jnp.bfloat16)
    filler = jnp.zeros((slots, SPAN - 3 * npredictors), jnp.bfloat16)
    aug = jnp.concatenate([main, main, rest, filler], axis=1)
    flip = jnp.concatenate([main, rest], axis=1).T

    def fixed(shape):
        return pl.BlockSpec(shape, lambda i: (0, 0))

    def moving(height):
        return pl.BlockSpec((height, tile), lambda i: (0, i))

    return pl.pallas_call(
        functools.partial(compute_kernel, block_len, scaling),
        grid=(channels // tile,),
        out_shape=(
            jax.ShapeDtypeStruct((slots, channels), jnp.bfloat16),
            jax.ShapeDtypeStruct((slots, profile_len), jnp.bfloat16),
            jax.ShapeDtypeStruct((npredictors, channels), jnp.float32),
        ),
        in_specs=[
            pl.BlockSpec(memory_space=pltpu.SMEM),
            fixed((slots, profile_len)),
            fixed((slots, SPAN)),
            fixed((2 * npredictors, slots)),
            moving(profile_len),
            moving(slots),
            moving(npredictors),
            moving(1),
        ],
        out_specs=(moving(slots), fixed((slots, profile_len)), moving(npredictors)),
        scratch_shapes=[
            pltpu.VMEM((slots, profile_len + SPAN), jnp.bfloat16),
            pltpu.VMEM((slots, profile_len), jnp.float32),
            pltpu.VMEM((slots, tile), jnp.bfloat16),
            pltpu.VMEM((slots, tile), jnp.bfloat16),
        ],
        compiler_params=pltpu.CompilerParams(vmem_limit_bytes=GRANT),
        name="operator",
    )(obs_count, pred, aug, flip, coef, dep, beta, weight)


def return_kernel(
    lat_count,
    lon_count,
    capacity,
    pulled_ref,
    position_ref,
    wanted_ref,
    bias_ref,
    base_ref,
    grad_ref,
    sum_ref,
    outbound,
    inbound,
    shares,
    collector,
    jacobian,
    row_send,
    row_recv,
    bias_send,
    bias_recv,
):
    devices = lat_count * lon_count
    column_count, profile_len = base_ref.shape
    slots = pulled_ref.shape[0]
    rows = devices * capacity
    me, peer = peers_of(lat_count, lon_count)
    barrier = greet(devices, peer)
    placed = ones_where(iota((rows, slots), 0) == position_ref[...])
    payload = dot(placed, pulled_ref[...]).reshape(devices, capacity, profile_len)
    outbound[...] = payload.astype(jnp.bfloat16)
    pl.semaphore_wait(barrier, devices - 1)
    send_all(devices, me, peer, outbound, inbound, row_send, row_recv)
    send_all(devices, me, peer, bias_ref, shares, bias_send, bias_recv)
    inbound[me] = outbound[me]
    shares[me] = bias_ref[me]
    collector[...] = ones_where(iota((column_count, rows), 0) == wanted_ref[...])
    jacobian[...] = 1.0 + 0.5 * jnp.tanh(base_ref[...].astype(jnp.float32))
    wait_all(devices, peer, outbound, inbound, row_send, row_recv)
    arrived = inbound[...].astype(jnp.float32).reshape(rows, profile_len).astype(jnp.bfloat16)
    grad_ref[...] = (dot(collector[...], arrived) * jacobian[...]).astype(jnp.bfloat16)
    wait_all(devices, peer, bias_ref, shares, bias_send, bias_recv)
    sum_ref[...] = jnp.sum(shares[...], axis=0)


def give_back(lat_count, lon_count, capacity, pulled, position, wanted, bias, background):
    devices = lat_count * lon_count
    column_count, profile_len = background.shape
    rows = devices * capacity
    return pl.pallas_call(
        functools.partial(return_kernel, lat_count, lon_count, capacity),
        out_shape=(
            jax.ShapeDtypeStruct(background.shape, jnp.bfloat16),
            jax.ShapeDtypeStruct(bias.shape[1:], jnp.float32),
        ),
        in_specs=[VMEM] * 5,
        out_specs=(VMEM,) * 2,
        scratch_shapes=[
            pltpu.VMEM((devices, capacity, profile_len), jnp.bfloat16),
            pltpu.VMEM((devices, capacity, profile_len), jnp.bfloat16),
            pltpu.VMEM(bias.shape, jnp.float32),
            pltpu.VMEM((column_count, rows), jnp.bfloat16),
            pltpu.VMEM((column_count, profile_len), jnp.float32),
        ]
        + [pltpu.SemaphoreType.DMA((devices,))] * 4,
        compiler_params=pltpu.CompilerParams(
            collective_id=1, has_side_effects=True, vmem_limit_bytes=GRANT
        ),
        name="return_adjoint",
    )(pulled, position, wanted, bias, background)


def shards(
    background,
    increment,
    coefficients,
    departures,
    bias_pred,
    beta_incr,
    obs_weight,
    obs_count,
    col_index,
):
    lat_count = lax.axis_size("lat")
    lon_count = lax.axis_size("lon")
    devices = lat_count * lon_count
    block_count, block_len = col_index.shape
    channels = coefficients.shape[1]
    npredictors = bias_pred.shape[2]
    slot_count = block_count * block_len
    capacity = 8 * pl.cdiv(3 * slot_count // (2 * devices), 8)
    scaling = (slot_count * devices) ** -0.5
    pred, position, wanted = fetch(
        lat_count, lon_count, capacity, col_index.reshape(1, slot_count), background, increment
    )
    radiance, pulled, bias = compute(
        block_len,
        scaling,
        obs_count,
        pred,
        bias_pred.reshape(slot_count, npredictors),
        coefficients,
        departures.reshape(slot_count, channels),
        beta_incr,
        obs_weight.reshape(1, channels),
    )
    bias = bias.reshape(npredictors, devices, channels // devices).transpose(1, 0, 2)
    column_grad, bias_grad = give_back(
        lat_count, lon_count, capacity, pulled, position, wanted, bias, background
    )
    return (radiance.reshape(departures.shape), column_grad, bias_grad.T)


def solution(mesh):
    return jax.shard_map(
        shards,
        mesh=mesh,
        in_specs=(
            P(("lat", "lon"), None),
            P(("lat", "lon"), None),
            P(),
            P(("lat", "lon"), None, None),
            P(("lat", "lon"), None, None),
            P(),
            P(),
            P(("lat", "lon")),
            P(("lat", "lon"), None),
        ),
        out_specs=(P(("lat", "lon"), None, None), P(("lat", "lon"), None), P(("lat", "lon"), None)),
        check_vma=False,
    )
```

```python
import functools

import jax
import jax.numpy as jnp
from jax import lax
from jax.experimental import pallas as pl
from jax.experimental.pallas import tpu as pltpu
from jax.sharding import PartitionSpec as P

MESH = pl.DeviceIdType.MESH
VMEM = pl.BlockSpec(memory_space=pltpu.VMEM)
SPAN = 128
GRANT = 60 * 1024 * 1024


def peers_of(lat_count, lon_count):
    devices = lat_count * lon_count
    me = lax.axis_index("lat") * lon_count + lax.axis_index("lon")

    def peer(offset):
        other = lax.rem(me + offset, devices)
        return other, (lax.div(other, lon_count), lax.rem(other, lon_count))

    return me, peer


def greet(devices, peer):
    barrier = pltpu.get_barrier_semaphore()

    def one(offset, carry):
        pl.semaphore_signal(barrier, inc=1, device_id=peer(offset)[1], device_id_type=MESH)
        return carry

    lax.fori_loop(1, devices, one, 0)
    return barrier


def send_all(devices, me, peer, source, target, send_sem, recv_sem):
    def one(offset, carry):
        other, where = peer(offset)
        pltpu.make_async_remote_copy(
            src_ref=source.at[other],
            dst_ref=target.at[me],
            send_sem=send_sem.at[offset],
            recv_sem=recv_sem.at[me],
            device_id=where,
            device_id_type=MESH,
        ).start()
        return carry

    lax.fori_loop(1, devices, one, 0)


def wait_all(devices, peer, source, target, send_sem, recv_sem):
    def one(offset, carry):
        other, where = peer(offset)
        copy = pltpu.make_async_remote_copy(
            src_ref=source.at[other],
            dst_ref=target.at[other],
            send_sem=send_sem.at[offset],
            recv_sem=recv_sem.at[other],
            device_id=where,
            device_id_type=MESH,
        )
        copy.wait_recv()
        copy.wait_send()
        return carry

    lax.fori_loop(1, devices, one, 0)


def iota(shape, dim):
    return lax.broadcasted_iota(jnp.int32, shape, dim)


def ones_where(mask):
    return jnp.where(mask, jnp.float32(1.0), jnp.float32(0.0)).astype(jnp.bfloat16)


def dot(a, b):
    return jnp.dot(a, b, preferred_element_type=jnp.float32)


def dot_nt(a, b):
    return lax.dot_general(a, b, (((1,), (1,)), ((), ())), preferred_element_type=jnp.float32)


def fetch_kernel(
    lat_count,
    lon_count,
    capacity,
    cols_ref,
    base_ref,
    step_ref,
    pred_ref,
    position_ref,
    wanted_ref,
    ask,
    asked,
    formed,
    outbound,
    inbound,
    picker,
    ask_send,
    ask_recv,
    row_send,
    row_recv,
):
    devices = lat_count * lon_count
    column_count, profile_len = base_ref.shape
    slots = cols_ref.shape[1]
    rows = devices * capacity
    shift = column_count.bit_length() - 1
    assert column_count == 1 << shift
    me, peer = peers_of(lat_count, lon_count)
    barrier = greet(devices, peer)

    cols = cols_ref[...]
    owners = lax.shift_right_logical(cols, shift)
    local = cols & (column_count - 1)
    owned = jnp.where(iota((devices, slots), 0) == owners, jnp.float32(1.0), jnp.float32(0.0))
    before = ones_where(iota((slots, slots), 0) < iota((slots, slots), 1))
    ranks = dot(owned.astype(jnp.bfloat16), before)
    rank = jnp.sum(owned * ranks, axis=0, keepdims=True).astype(jnp.int32)
    position = owners * capacity + rank
    position_ref[...] = position
    spot = ones_where(iota((SPAN, slots), 0) == rank)
    high = lax.shift_right_logical(local, 8).astype(jnp.float32)
    low = (local & 255).astype(jnp.float32)
    asks = dot_nt((owned * high).astype(jnp.bfloat16), spot) * 256.0
    asks = asks + dot_nt((owned * low).astype(jnp.bfloat16), spot)
    ask[:, 0, :] = asks

    pl.semaphore_wait(barrier, devices - 1)
    send_all(devices, me, peer, ask, asked, ask_send, ask_recv)
    asked[me] = ask[me]
    jacobian = 1.0 + 0.5 * jnp.tanh(base_ref[...].astype(jnp.float32))
    formed[...] = (step_ref[...].astype(jnp.float32) * jacobian).astype(jnp.bfloat16)
    wait_all(devices, peer, ask, asked, ask_send, ask_recv)

    table = asked[:, 0, :].astype(jnp.int32)
    first = iota((rows, devices), 1) * capacity
    row = iota((rows, devices), 0)
    spread = ones_where((row >= first) & (row < first + capacity))
    table_high = lax.shift_right_logical(table, 8).astype(jnp.float32).astype(jnp.bfloat16)
    table_low = (table & 255).astype(jnp.float32).astype(jnp.bfloat16)
    listed = dot(spread, table_high) * 256.0 + dot(spread, table_low)
    row_f = iota((rows, SPAN), 0).astype(jnp.float32)
    within = row_f - capacity * jnp.floor((row_f + 0.5) * (1.0 / capacity))
    lane_f = iota((rows, SPAN), 1).astype(jnp.float32)
    wanted = jnp.sum(jnp.where(lane_f == within, listed, 0.0), axis=1, keepdims=True)
    wanted = wanted.astype(jnp.int32)
    chosen = ones_where(wanted == iota((rows, column_count), 1))
    payload = dot(chosen, formed[...]).reshape(devices, capacity, profile_len)
    outbound[...] = payload.astype(jnp.bfloat16)
    send_all(devices, me, peer, outbound, inbound, row_send, row_recv)
    inbound[me] = outbound[me]

    diagonal = iota((rows, rows), 0) == iota((rows, rows), 1)
    wanted_f = wanted.astype(jnp.float32)
    wanted_ref[...] = jnp.sum(
        jnp.where(diagonal, wanted_f, 0.0), axis=0, keepdims=True
    ).astype(jnp.int32)
    diagonal = iota((slots, slots), 0) == iota((slots, slots), 1)
    upright = jnp.sum(
        jnp.where(diagonal, position.astype(jnp.float32), 0.0), axis=1, keepdims=True
    ).astype(jnp.int32)
    picker[...] = ones_where(upright == iota((slots, rows), 1))
    wait_all(devices, peer, outbound, inbound, row_send, row_recv)
    arrived = inbound[...].astype(jnp.float32).reshape(rows, profile_len).astype(jnp.bfloat16)
    pred_ref[...] = dot(picker[...], arrived).astype(jnp.bfloat16)


def fetch(lat_count, lon_count, capacity, cols, background, increment):
    devices = lat_count * lon_count
    column_count, profile_len = background.shape
    slots = cols.shape[1]
    rows = devices * capacity
    return pl.pallas_call(
        functools.partial(fetch_kernel, lat_count, lon_count, capacity),
        out_shape=(
            jax.ShapeDtypeStruct((slots, profile_len), jnp.bfloat16),
            jax.ShapeDtypeStruct((1, slots), jnp.int32),
            jax.ShapeDtypeStruct((1, rows), jnp.int32),
        ),
        in_specs=[VMEM] * 3,
        out_specs=(VMEM,) * 3,
        scratch_shapes=[
            pltpu.VMEM((devices, 1, SPAN), jnp.float32),
            pltpu.VMEM((devices, 1, SPAN), jnp.float32),
            pltpu.VMEM((column_count, profile_len), jnp.bfloat16),
            pltpu.VMEM((devices, capacity, profile_len), jnp.bfloat16),
            pltpu.VMEM((devices, capacity, profile_len), jnp.bfloat16),
            pltpu.VMEM((slots, rows), jnp.bfloat16),
        ]
        + [pltpu.SemaphoreType.DMA((devices,))] * 4,
        compiler_params=pltpu.CompilerParams(
            collective_id=0, has_side_effects=True, vmem_limit_bytes=GRANT
        ),
        name="fetch_profiles",
    )(cols, background, increment)


def compute_kernel(
    block_len,
    scaling,
    count_ref,
    pred_ref,
    side_ref,
    coef_ref,
    dep_ref,
    beta_ref,
    weight_ref,
    rad_ref,
    pulled_ref,
    bias_ref,
    left,
    flip,
    total,
    product,
    main,
    rest,
):
    step = pl.program_id(0)
    profile_len = pred_ref.shape[1]
    npredictors, tile = beta_ref.shape

    @pl.when(step == 0)
    def _():
        left[:, :profile_len] = pred_ref[...]
        side = side_ref[...]
        side_main = side.astype(jnp.bfloat16).astype(jnp.float32)
        side_rest = side - side_main
        flip[...] = jnp.concatenate([side_main, side_rest], axis=0).astype(jnp.bfloat16)
        blank = jnp.zeros((SPAN - 3 * npredictors, side.shape[1]), jnp.float32)
        stack = jnp.concatenate([side_main, side_main, side_rest, blank], axis=0)
        left[:, profile_len:] = stack.T.astype(jnp.bfloat16)
        total[...] = jnp.zeros_like(total)

    coef = coef_ref[...]
    beta = beta_ref[...]
    beta_main = beta.astype(jnp.bfloat16).astype(jnp.float32)
    beta_rest = beta - beta_main
    filler = jnp.zeros((SPAN - 3 * npredictors, tile), jnp.float32)
    extra = jnp.concatenate([beta_main, beta_rest, beta_main, filler], axis=0)
    right = jnp.concatenate([coef, extra.astype(jnp.bfloat16)], axis=0)
    weight = weight_ref[...]
    product[...] = dot(left[...], right)
    for block in range(pred_ref.shape[0] // block_len):
        part = pl.ds(block * block_len, block_len)
        present = iota((block_len, tile), 0) < count_ref[block]
        radiance = jnp.where(present, product[part, :], 0.0)
        rad_ref[part, :] = radiance.astype(jnp.bfloat16)
        misfit = weight * (radiance - dep_ref[part, :].astype(jnp.float32))
        misfit = jnp.where(present, misfit, 0.0)
        misfit_b = misfit.astype(jnp.bfloat16)
        main[part, :] = misfit_b
        rest[part, :] = (misfit - misfit_b.astype(jnp.float32)).astype(jnp.bfloat16)
    total[...] += dot_nt(main[...], coef)
    whole = dot(flip[...], main[...])
    small = dot(flip[...], rest[...])
    bias_ref[...] = scaling * (
        whole[:npredictors] + whole[npredictors:] + small[:npredictors]
    )

    @pl.when(step == pl.num_programs(0) - 1)
    def _():
        pulled_ref[...] = total[...].astype(jnp.bfloat16)


def compute(block_len, scaling, obs_count, pred, side, coef, dep, beta, weight):
    slots, profile_len = pred.shape
    channels = coef.shape[1]
    npredictors = side.shape[0]
    tile = max(t for t in range(128, 513, 128) if channels % t == 0)
    def fixed(shape):
        return pl.BlockSpec(shape, lambda i: (0, 0))

    def moving(height):
        return pl.BlockSpec((height, tile), lambda i: (0, i))

    return pl.pallas_call(
        functools.partial(compute_kernel, block_len, scaling),
        grid=(channels // tile,),
        out_shape=(
            jax.ShapeDtypeStruct((slots, channels), jnp.bfloat16),
            jax.ShapeDtypeStruct((slots, profile_len), jnp.bfloat16),
            jax.ShapeDtypeStruct((npredictors, channels), jnp.float32),
        ),
        in_specs=[
            pl.BlockSpec(memory_space=pltpu.SMEM),
            fixed((slots, profile_len)),
            fixed((npredictors, slots)),
            moving(profile_len),
            moving(slots),
            moving(npredictors),
            moving(1),
        ],
        out_specs=(moving(slots), fixed((slots, profile_len)), moving(npredictors)),
        scratch_shapes=[
            pltpu.VMEM((slots, profile_len + SPAN), jnp.bfloat16),
            pltpu.VMEM((2 * npredictors, slots), jnp.bfloat16),
            pltpu.VMEM((slots, profile_len), jnp.float32),
            pltpu.VMEM((slots, tile), jnp.float32),
            pltpu.VMEM((slots, tile), jnp.bfloat16),
            pltpu.VMEM((slots, tile), jnp.bfloat16),
        ],
        compiler_params=pltpu.CompilerParams(vmem_limit_bytes=GRANT),
        name="operator",
    )(obs_count, pred, side, coef, dep, beta, weight)


def return_kernel(
    lat_count,
    lon_count,
    capacity,
    pulled_ref,
    position_ref,
    wanted_ref,
    bias_ref,
    base_ref,
    grad_ref,
    sum_ref,
    outbound,
    inbound,
    shares,
    collector,
    jacobian,
    row_send,
    row_recv,
    bias_send,
    bias_recv,
):
    devices = lat_count * lon_count
    column_count, profile_len = base_ref.shape
    slots = pulled_ref.shape[0]
    rows = devices * capacity
    me, peer = peers_of(lat_count, lon_count)
    barrier = greet(devices, peer)
    placed = ones_where(iota((rows, slots), 0) == position_ref[...])
    payload = dot(placed, pulled_ref[...]).reshape(devices, capacity, profile_len)
    outbound[...] = payload.astype(jnp.bfloat16)
    pl.semaphore_wait(barrier, devices - 1)
    send_all(devices, me, peer, outbound, inbound, row_send, row_recv)
    send_all(devices, me, peer, bias_ref, shares, bias_send, bias_recv)
    inbound[me] = outbound[me]
    shares[me] = bias_ref[me]
    collector[...] = ones_where(iota((column_count, rows), 0) == wanted_ref[...])
    jacobian[...] = 1.0 + 0.5 * jnp.tanh(base_ref[...].astype(jnp.float32))
    wait_all(devices, peer, outbound, inbound, row_send, row_recv)
    arrived = inbound[...].astype(jnp.float32).reshape(rows, profile_len).astype(jnp.bfloat16)
    grad_ref[...] = (dot(collector[...], arrived) * jacobian[...]).astype(jnp.bfloat16)
    wait_all(devices, peer, bias_ref, shares, bias_send, bias_recv)
    sum_ref[...] = jnp.sum(shares[...].astype(jnp.float32), axis=0)


def give_back(lat_count, lon_count, capacity, pulled, position, wanted, bias, background):
    devices = lat_count * lon_count
    column_count, profile_len = background.shape
    rows = devices * capacity
    return pl.pallas_call(
        functools.partial(return_kernel, lat_count, lon_count, capacity),
        out_shape=(
            jax.ShapeDtypeStruct(background.shape, jnp.bfloat16),
            jax.ShapeDtypeStruct(bias.shape[1:], jnp.float32),
        ),
        in_specs=[VMEM] * 5,
        out_specs=(VMEM,) * 2,
        scratch_shapes=[
            pltpu.VMEM((devices, capacity, profile_len), jnp.bfloat16),
            pltpu.VMEM((devices, capacity, profile_len), jnp.bfloat16),
            pltpu.VMEM(bias.shape, bias.dtype),
            pltpu.VMEM((column_count, rows), jnp.bfloat16),
            pltpu.VMEM((column_count, profile_len), jnp.float32),
        ]
        + [pltpu.SemaphoreType.DMA((devices,))] * 4,
        compiler_params=pltpu.CompilerParams(
            collective_id=1, has_side_effects=True, vmem_limit_bytes=GRANT
        ),
        name="return_adjoint",
    )(pulled, position, wanted, bias, background)


def shards(
    background,
    increment,
    coefficients,
    departures,
    bias_pred,
    beta_incr,
    obs_weight,
    obs_count,
    col_index,
):
    lat_count = lax.axis_size("lat")
    lon_count = lax.axis_size("lon")
    devices = lat_count * lon_count
    block_count, block_len = col_index.shape
    channels = coefficients.shape[1]
    npredictors = bias_pred.shape[2]
    slot_count = block_count * block_len
    capacity = 8 * pl.cdiv(3 * slot_count // (2 * devices), 8)
    scaling = (slot_count * devices) ** -0.5
    pred, position, wanted = fetch(
        lat_count, lon_count, capacity, col_index.reshape(1, slot_count), background, increment
    )
    radiance, pulled, bias = compute(
        block_len,
        scaling,
        obs_count,
        pred,
        bias_pred.reshape(slot_count, npredictors).T,
        coefficients,
        departures.reshape(slot_count, channels),
        beta_incr,
        obs_weight.reshape(1, channels),
    )
    bias = bias.astype(jnp.bfloat16).reshape(npredictors, devices, channels // devices).transpose(1, 0, 2)
    column_grad, bias_grad = give_back(
        lat_count, lon_count, capacity, pulled, position, wanted, bias, background
    )
    return (radiance.reshape(departures.shape), column_grad, bias_grad.T)


def solution(mesh):
    return jax.shard_map(
        shards,
        mesh=mesh,
        in_specs=(
            P(("lat", "lon"), None),
            P(("lat", "lon"), None),
            P(),
            P(("lat", "lon"), None, None),
            P(("lat", "lon"), None, None),
            P(),
            P(),
            P(("lat", "lon")),
            P(("lat", "lon"), None),
        ),
        out_specs=(P(("lat", "lon"), None, None), P(("lat", "lon"), None), P(("lat", "lon"), None)),
        check_vma=False,
    )
```

```python
import functools
import math

import jax
import jax.numpy as jnp
from jax import lax
from jax.experimental import pallas as pl
from jax.experimental.pallas import tpu as pltpu
from jax.sharding import PartitionSpec as P

MESH = pl.DeviceIdType.MESH
VMEM = pl.BlockSpec(memory_space=pltpu.VMEM)
SPAN = 128
GRANT = 60 * 1024 * 1024


def peers_of(lat_count, lon_count):
    devices = lat_count * lon_count
    me = lax.axis_index("lat") * lon_count + lax.axis_index("lon")
    stride = next(s for s in range(lon_count + 3, devices + lon_count + 4) if math.gcd(s, devices) == 1)

    def peer(offset):
        other = lax.rem(me + offset * stride, devices)
        return other, (lax.div(other, lon_count), lax.rem(other, lon_count))

    return me, peer


def greet(devices, peer):
    barrier = pltpu.get_barrier_semaphore()

    def one(offset, carry):
        pl.semaphore_signal(barrier, inc=1, device_id=peer(offset)[1], device_id_type=MESH)
        return carry

    lax.fori_loop(1, devices, one, 0)
    return barrier


def send_all(devices, me, peer, source, target, send_sem, recv_sem):
    def one(offset, carry):
        other, where = peer(offset)
        pltpu.make_async_remote_copy(
            src_ref=source.at[other],
            dst_ref=target.at[me],
            send_sem=send_sem.at[offset],
            recv_sem=recv_sem.at[me],
            device_id=where,
            device_id_type=MESH,
        ).start()
        return carry

    lax.fori_loop(1, devices, one, 0)


def wait_all(devices, peer, source, target, send_sem, recv_sem):
    def one(offset, carry):
        other, where = peer(offset)
        copy = pltpu.make_async_remote_copy(
            src_ref=source.at[other],
            dst_ref=target.at[other],
            send_sem=send_sem.at[offset],
            recv_sem=recv_sem.at[other],
            device_id=where,
            device_id_type=MESH,
        )
        copy.wait_recv()
        copy.wait_send()
        return carry

    lax.fori_loop(1, devices, one, 0)


def iota(shape, dim):
    return lax.broadcasted_iota(jnp.int32, shape, dim)


def ones_where(mask):
    return jnp.where(mask, jnp.float32(1.0), jnp.float32(0.0)).astype(jnp.bfloat16)


def dot(a, b):
    return jnp.dot(a, b, preferred_element_type=jnp.float32)


def dot_nt(a, b):
    return lax.dot_general(a, b, (((1,), (1,)), ((), ())), preferred_element_type=jnp.float32)


def fetch_kernel(
    lat_count,
    lon_count,
    capacity,
    cols_ref,
    base_ref,
    step_ref,
    pred_ref,
    position_ref,
    wanted_ref,
    ask,
    asked,
    formed,
    outbound,
    inbound,
    picker,
    ask_send,
    ask_recv,
    row_send,
    row_recv,
):
    devices = lat_count * lon_count
    column_count, profile_len = base_ref.shape
    slots = cols_ref.shape[1]
    rows = devices * capacity
    shift = column_count.bit_length() - 1
    assert column_count == 1 << shift
    me, peer = peers_of(lat_count, lon_count)
    barrier = greet(devices, peer)

    cols = cols_ref[...]
    owners = lax.shift_right_logical(cols, shift)
    local = cols & (column_count - 1)
    owned = jnp.where(iota((devices, slots), 0) == owners, jnp.float32(1.0), jnp.float32(0.0))
    before = ones_where(iota((slots, slots), 0) < iota((slots, slots), 1))
    ranks = dot(owned.astype(jnp.bfloat16), before)
    rank = jnp.sum(owned * ranks, axis=0, keepdims=True).astype(jnp.int32)
    position = owners * capacity + rank
    position_ref[...] = position
    spot = ones_where(iota((SPAN, slots), 0) == rank)
    high = lax.shift_right_logical(local, 8).astype(jnp.float32)
    low = (local & 255).astype(jnp.float32)
    asks = dot_nt((owned * high).astype(jnp.bfloat16), spot) * 256.0
    asks = asks + dot_nt((owned * low).astype(jnp.bfloat16), spot)
    ask[:, 0, :] = asks

    pl.semaphore_wait(barrier, devices - 1)
    send_all(devices, me, peer, ask, asked, ask_send, ask_recv)
    asked[me] = ask[me]
    jacobian = 1.0 + 0.5 * jnp.tanh(base_ref[...].astype(jnp.float32))
    formed[...] = (step_ref[...].astype(jnp.float32) * jacobian).astype(jnp.bfloat16)
    wait_all(devices, peer, ask, asked, ask_send, ask_recv)

    table = asked[:, 0, :].astype(jnp.int32)
    first = iota((rows, devices), 1) * capacity
    row = iota((rows, devices), 0)
    spread = ones_where((row >= first) & (row < first + capacity))
    table_high = lax.shift_right_logical(table, 8).astype(jnp.float32).astype(jnp.bfloat16)
    table_low = (table & 255).astype(jnp.float32).astype(jnp.bfloat16)
    listed = dot(spread, table_high) * 256.0 + dot(spread, table_low)
    row_f = iota((rows, SPAN), 0).astype(jnp.float32)
    within = row_f - capacity * jnp.floor((row_f + 0.5) * (1.0 / capacity))
    lane_f = iota((rows, SPAN), 1).astype(jnp.float32)
    wanted = jnp.sum(jnp.where(lane_f == within, listed, 0.0), axis=1, keepdims=True)
    wanted = wanted.astype(jnp.int32)
    chosen = ones_where(wanted == iota((rows, column_count), 1))
    payload = dot(chosen, formed[...]).reshape(devices, capacity, profile_len)
    outbound[...] = payload.astype(jnp.bfloat16)
    send_all(devices, me, peer, outbound, inbound, row_send, row_recv)
    inbound[me] = outbound[me]

    diagonal = iota((rows, rows), 0) == iota((rows, rows), 1)
    wanted_f = wanted.astype(jnp.float32)
    wanted_ref[...] = jnp.sum(
        jnp.where(diagonal, wanted_f, 0.0), axis=0, keepdims=True
    ).astype(jnp.int32)
    diagonal = iota((slots, slots), 0) == iota((slots, slots), 1)
    upright = jnp.sum(
        jnp.where(diagonal, position.astype(jnp.float32), 0.0), axis=1, keepdims=True
    ).astype(jnp.int32)
    picker[...] = ones_where(upright == iota((slots, rows), 1))
    wait_all(devices, peer, outbound, inbound, row_send, row_recv)
    arrived = inbound[...].astype(jnp.float32).reshape(rows, profile_len).astype(jnp.bfloat16)
    pred_ref[...] = dot(picker[...], arrived).astype(jnp.bfloat16)


def fetch(lat_count, lon_count, capacity, cols, background, increment):
    devices = lat_count * lon_count
    column_count, profile_len = background.shape
    slots = cols.shape[1]
    rows = devices * capacity
    return pl.pallas_call(
        functools.partial(fetch_kernel, lat_count, lon_count, capacity),
        out_shape=(
            jax.ShapeDtypeStruct((slots, profile_len), jnp.bfloat16),
            jax.ShapeDtypeStruct((1, slots), jnp.int32),
            jax.ShapeDtypeStruct((1, rows), jnp.int32),
        ),
        in_specs=[VMEM] * 3,
        out_specs=(VMEM,) * 3,
        scratch_shapes=[
            pltpu.VMEM((devices, 1, SPAN), jnp.float32),
            pltpu.VMEM((devices, 1, SPAN), jnp.float32),
            pltpu.VMEM((column_count, profile_len), jnp.bfloat16),
            pltpu.VMEM((devices, capacity, profile_len), jnp.bfloat16),
            pltpu.VMEM((devices, capacity, profile_len), jnp.bfloat16),
            pltpu.VMEM((slots, rows), jnp.bfloat16),
        ]
        + [pltpu.SemaphoreType.DMA((devices,))] * 4,
        compiler_params=pltpu.CompilerParams(
            collective_id=0, has_side_effects=True, vmem_limit_bytes=GRANT
        ),
        name="fetch_profiles",
    )(cols, background, increment)


def compute_kernel(
    block_len,
    scaling,
    count_ref,
    pred_ref,
    side_ref,
    coef_ref,
    dep_ref,
    beta_ref,
    weight_ref,
    rad_ref,
    pulled_ref,
    bias_ref,
    left,
    flip,
    total,
    main,
    rest,
):
    step = pl.program_id(0)
    profile_len = pred_ref.shape[1]
    npredictors, tile = beta_ref.shape

    @pl.when(step == 0)
    def _():
        left[:, :profile_len] = pred_ref[...]
        side = side_ref[...]
        side_main = side.astype(jnp.bfloat16).astype(jnp.float32)
        side_rest = side - side_main
        flip[...] = jnp.concatenate([side_main, side_rest], axis=0).astype(jnp.bfloat16)
        blank = jnp.zeros((SPAN - 3 * npredictors, side.shape[1]), jnp.float32)
        stack = jnp.concatenate([side_main, side_main, side_rest, blank], axis=0)
        left[:, profile_len:] = stack.T.astype(jnp.bfloat16)
        total[...] = jnp.zeros_like(total)

    coef = coef_ref[...]
    beta = beta_ref[...]
    beta_main = beta.astype(jnp.bfloat16).astype(jnp.float32)
    beta_rest = beta - beta_main
    filler = jnp.zeros((SPAN - 3 * npredictors, tile), jnp.float32)
    extra = jnp.concatenate([beta_main, beta_rest, beta_main, filler], axis=0)
    right = jnp.concatenate([coef, extra.astype(jnp.bfloat16)], axis=0)
    weight = weight_ref[...]
    for block in range(pred_ref.shape[0] // block_len):
        part = pl.ds(block * block_len, block_len)
        present = iota((block_len, tile), 0) < count_ref[block]
        radiance = jnp.where(present, dot(left[part, :], right), 0.0)
        rad_ref[part, :] = radiance.astype(jnp.bfloat16)
        misfit = weight * (radiance - dep_ref[part, :].astype(jnp.float32))
        misfit = jnp.where(present, misfit, 0.0)
        misfit_b = misfit.astype(jnp.bfloat16)
        main[part, :] = misfit_b
        rest[part, :] = (misfit - misfit_b.astype(jnp.float32)).astype(jnp.bfloat16)
    total[...] += dot_nt(main[...], coef)
    whole = dot(flip[...], main[...])
    small = dot(flip[...], rest[...])
    share = whole[:npredictors] + whole[npredictors:] + small[:npredictors]
    bias_ref[...] = (scaling * share).astype(bias_ref.dtype)

    @pl.when(step == pl.num_programs(0) - 1)
    def _():
        pulled_ref[...] = total[...].astype(jnp.bfloat16)


def compute(block_len, scaling, obs_count, pred, side, coef, dep, beta, weight):
    slots, profile_len = pred.shape
    channels = coef.shape[1]
    npredictors = side.shape[0]
    tile = max(t for t in range(128, 513, 128) if channels % t == 0)
    def fixed(shape):
        return pl.BlockSpec(shape, lambda i: (0, 0))

    def moving(height):
        return pl.BlockSpec((height, tile), lambda i: (0, i))

    return pl.pallas_call(
        functools.partial(compute_kernel, block_len, scaling),
        grid=(channels // tile,),
        out_shape=(
            jax.ShapeDtypeStruct((slots, channels), jnp.bfloat16),
            jax.ShapeDtypeStruct((slots, profile_len), jnp.bfloat16),
            jax.ShapeDtypeStruct((npredictors, channels), jnp.bfloat16),
        ),
        in_specs=[
            pl.BlockSpec(memory_space=pltpu.SMEM),
            fixed((slots, profile_len)),
            fixed((npredictors, slots)),
            moving(profile_len),
            moving(slots),
            moving(npredictors),
            moving(1),
        ],
        out_specs=(moving(slots), fixed((slots, profile_len)), moving(npredictors)),
        scratch_shapes=[
            pltpu.VMEM((slots, profile_len + SPAN), jnp.bfloat16),
            pltpu.VMEM((2 * npredictors, slots), jnp.bfloat16),
            pltpu.VMEM((slots, profile_len), jnp.float32),
            pltpu.VMEM((slots, tile), jnp.bfloat16),
            pltpu.VMEM((slots, tile), jnp.bfloat16),
        ],
        compiler_params=pltpu.CompilerParams(vmem_limit_bytes=GRANT),
        name="operator",
    )(obs_count, pred, side, coef, dep, beta, weight)


def return_kernel(
    lat_count,
    lon_count,
    capacity,
    pulled_ref,
    position_ref,
    wanted_ref,
    bias_ref,
    base_ref,
    grad_ref,
    sum_ref,
    outbound,
    inbound,
    shares,
    collector,
    jacobian,
    row_send,
    row_recv,
    bias_send,
    bias_recv,
):
    devices = lat_count * lon_count
    column_count, profile_len = base_ref.shape
    slots = pulled_ref.shape[0]
    rows = devices * capacity
    me, peer = peers_of(lat_count, lon_count)
    barrier = greet(devices, peer)
    placed = ones_where(iota((rows, slots), 0) == position_ref[...])
    payload = dot(placed, pulled_ref[...]).reshape(devices, capacity, profile_len)
    outbound[...] = payload.astype(jnp.bfloat16)
    pl.semaphore_wait(barrier, devices - 1)
    send_all(devices, me, peer, outbound, inbound, row_send, row_recv)
    send_all(devices, me, peer, bias_ref, shares, bias_send, bias_recv)
    inbound[me] = outbound[me]
    shares[me] = bias_ref[me]
    collector[...] = ones_where(iota((column_count, rows), 0) == wanted_ref[...])
    jacobian[...] = 1.0 + 0.5 * jnp.tanh(base_ref[...].astype(jnp.float32))
    wait_all(devices, peer, outbound, inbound, row_send, row_recv)
    arrived = inbound[...].astype(jnp.float32).reshape(rows, profile_len).astype(jnp.bfloat16)
    grad_ref[...] = (dot(collector[...], arrived) * jacobian[...]).astype(jnp.bfloat16)
    wait_all(devices, peer, bias_ref, shares, bias_send, bias_recv)
    sum_ref[...] = jnp.sum(shares[...].astype(jnp.float32), axis=0)


def give_back(lat_count, lon_count, capacity, pulled, position, wanted, bias, background):
    devices = lat_count * lon_count
    column_count, profile_len = background.shape
    rows = devices * capacity
    return pl.pallas_call(
        functools.partial(return_kernel, lat_count, lon_count, capacity),
        out_shape=(
            jax.ShapeDtypeStruct(background.shape, jnp.bfloat16),
            jax.ShapeDtypeStruct(bias.shape[1:], jnp.float32),
        ),
        in_specs=[VMEM] * 5,
        out_specs=(VMEM,) * 2,
        scratch_shapes=[
            pltpu.VMEM((devices, capacity, profile_len), jnp.bfloat16),
            pltpu.VMEM((devices, capacity, profile_len), jnp.bfloat16),
            pltpu.VMEM(bias.shape, bias.dtype),
            pltpu.VMEM((column_count, rows), jnp.bfloat16),
            pltpu.VMEM((column_count, profile_len), jnp.float32),
        ]
        + [pltpu.SemaphoreType.DMA((devices,))] * 4,
        compiler_params=pltpu.CompilerParams(
            collective_id=1, has_side_effects=True, vmem_limit_bytes=GRANT
        ),
        name="return_adjoint",
    )(pulled, position, wanted, bias, background)


def shards(
    background,
    increment,
    coefficients,
    departures,
    bias_pred,
    beta_incr,
    obs_weight,
    obs_count,
    col_index,
):
    lat_count = lax.axis_size("lat")
    lon_count = lax.axis_size("lon")
    devices = lat_count * lon_count
    block_count, block_len = col_index.shape
    channels = coefficients.shape[1]
    npredictors = bias_pred.shape[2]
    slot_count = block_count * block_len
    capacity = 8 * pl.cdiv(3 * slot_count // (2 * devices), 8)
    scaling = (slot_count * devices) ** -0.5
    pred, position, wanted = fetch(
        lat_count, lon_count, capacity, col_index.reshape(1, slot_count), background, increment
    )
    radiance, pulled, bias = compute(
        block_len,
        scaling,
        obs_count,
        pred,
        bias_pred.reshape(slot_count, npredictors).T,
        coefficients,
        departures.reshape(slot_count, channels),
        beta_incr,
        obs_weight.reshape(1, channels),
    )
    bias = bias.reshape(npredictors, devices, channels // devices).transpose(1, 0, 2)
    column_grad, bias_grad = give_back(
        lat_count, lon_count, capacity, pulled, position, wanted, bias, background
    )
    return (radiance.reshape(departures.shape), column_grad, bias_grad.T)


def solution(mesh):
    return jax.shard_map(
        shards,
        mesh=mesh,
        in_specs=(
            P(("lat", "lon"), None),
            P(("lat", "lon"), None),
            P(),
            P(("lat", "lon"), None, None),
            P(("lat", "lon"), None, None),
            P(),
            P(),
            P(("lat", "lon")),
            P(("lat", "lon"), None),
        ),
        out_specs=(P(("lat", "lon"), None, None), P(("lat", "lon"), None), P(("lat", "lon"), None)),
        check_vma=False,
    )
```

```python
import functools

import jax
import jax.numpy as jnp
from jax import lax
from jax.experimental import pallas as pl
from jax.experimental.pallas import tpu as pltpu
from jax.sharding import PartitionSpec as P

MESH = pl.DeviceIdType.MESH
VMEM = pl.BlockSpec(memory_space=pltpu.VMEM)
SPAN = 128
GRANT = 60 * 1024 * 1024


def peers_of(lat_count, lon_count):
    devices = lat_count * lon_count
    me = lax.axis_index("lat") * lon_count + lax.axis_index("lon")

    def peer(offset):
        other = lax.rem(me + offset, devices)
        return other, (lax.div(other, lon_count), lax.rem(other, lon_count))

    return me, peer


def greet(devices, peer):
    barrier = pltpu.get_barrier_semaphore()

    def one(offset, carry):
        pl.semaphore_signal(barrier, inc=1, device_id=peer(offset)[1], device_id_type=MESH)
        return carry

    lax.fori_loop(1, devices, one, 0)
    return barrier


def send_all(devices, me, peer, source, target, send_sem, recv_sem):
    def one(offset, carry):
        other, where = peer(offset)
        pltpu.make_async_remote_copy(
            src_ref=source.at[other],
            dst_ref=target.at[me],
            send_sem=send_sem.at[offset],
            recv_sem=recv_sem.at[me],
            device_id=where,
            device_id_type=MESH,
        ).start()
        return carry

    lax.fori_loop(1, devices, one, 0)


def wait_all(devices, peer, source, target, send_sem, recv_sem):
    def one(offset, carry):
        other, where = peer(offset)
        copy = pltpu.make_async_remote_copy(
            src_ref=source.at[other],
            dst_ref=target.at[other],
            send_sem=send_sem.at[offset],
            recv_sem=recv_sem.at[other],
            device_id=where,
            device_id_type=MESH,
        )
        copy.wait_recv()
        copy.wait_send()
        return carry

    lax.fori_loop(1, devices, one, 0)


def iota(shape, dim):
    return lax.broadcasted_iota(jnp.int32, shape, dim)


def ones_where(mask):
    return jnp.where(mask, jnp.float32(1.0), jnp.float32(0.0)).astype(jnp.bfloat16)


def dot(a, b):
    return jnp.dot(a, b, preferred_element_type=jnp.float32)


def dot_nt(a, b):
    return lax.dot_general(a, b, (((1,), (1,)), ((), ())), preferred_element_type=jnp.float32)


def fetch_kernel(
    lat_count,
    lon_count,
    capacity,
    cols_ref,
    base_ref,
    step_ref,
    pred_ref,
    position_ref,
    wanted_ref,
    ask,
    asked,
    formed,
    outbound,
    inbound,
    picker,
    ask_send,
    ask_recv,
    row_send,
    row_recv,
):
    devices = lat_count * lon_count
    column_count, profile_len = base_ref.shape
    slots = cols_ref.shape[1]
    rows = devices * capacity
    shift = column_count.bit_length() - 1
    assert column_count == 1 << shift
    me, peer = peers_of(lat_count, lon_count)
    barrier = greet(devices, peer)

    cols = cols_ref[...]
    owners = lax.shift_right_logical(cols, shift)
    local = cols & (column_count - 1)
    owned = jnp.where(iota((devices, slots), 0) == owners, jnp.float32(1.0), jnp.float32(0.0))
    before = ones_where(iota((slots, slots), 0) < iota((slots, slots), 1))
    ranks = dot(owned.astype(jnp.bfloat16), before)
    rank = jnp.sum(owned * ranks, axis=0, keepdims=True).astype(jnp.int32)
    position = owners * capacity + rank
    position_ref[...] = position
    spot = ones_where(iota((SPAN, slots), 0) == rank)
    high = lax.shift_right_logical(local, 8).astype(jnp.float32)
    low = (local & 255).astype(jnp.float32)
    asks = dot_nt((owned * high).astype(jnp.bfloat16), spot) * 256.0
    asks = asks + dot_nt((owned * low).astype(jnp.bfloat16), spot)
    ask[:, 0, :] = asks

    pl.semaphore_wait(barrier, devices - 1)
    send_all(devices, me, peer, ask, asked, ask_send, ask_recv)
    asked[me] = ask[me]
    jacobian = 1.0 + 0.5 * jnp.tanh(base_ref[...].astype(jnp.float32))
    formed[...] = (step_ref[...].astype(jnp.float32) * jacobian).astype(jnp.bfloat16)
    wait_all(devices, peer, ask, asked, ask_send, ask_recv)

    table = asked[:, 0, :].astype(jnp.int32)
    first = iota((rows, devices), 1) * capacity
    row = iota((rows, devices), 0)
    spread = ones_where((row >= first) & (row < first + capacity))
    table_high = lax.shift_right_logical(table, 8).astype(jnp.float32).astype(jnp.bfloat16)
    table_low = (table & 255).astype(jnp.float32).astype(jnp.bfloat16)
    listed = dot(spread, table_high) * 256.0 + dot(spread, table_low)
    row_f = iota((rows, SPAN), 0).astype(jnp.float32)
    within = row_f - capacity * jnp.floor((row_f + 0.5) * (1.0 / capacity))
    lane_f = iota((rows, SPAN), 1).astype(jnp.float32)
    wanted = jnp.sum(jnp.where(lane_f == within, listed, 0.0), axis=1, keepdims=True)
    wanted = wanted.astype(jnp.int32)
    chosen = ones_where(wanted == iota((rows, column_count), 1))
    payload = dot(chosen, formed[...]).reshape(devices, capacity, profile_len)
    outbound[...] = payload.astype(jnp.bfloat16)
    send_all(devices, me, peer, outbound, inbound, row_send, row_recv)
    inbound[me] = outbound[me]

    diagonal = iota((rows, rows), 0) == iota((rows, rows), 1)
    wanted_f = wanted.astype(jnp.float32)
    wanted_ref[...] = jnp.sum(
        jnp.where(diagonal, wanted_f, 0.0), axis=0, keepdims=True
    ).astype(jnp.int32)
    diagonal = iota((slots, slots), 0) == iota((slots, slots), 1)
    upright = jnp.sum(
        jnp.where(diagonal, position.astype(jnp.float32), 0.0), axis=1, keepdims=True
    ).astype(jnp.int32)
    picker[...] = ones_where(upright == iota((slots, rows), 1))
    wait_all(devices, peer, outbound, inbound, row_send, row_recv)
    arrived = inbound[...].astype(jnp.float32).reshape(rows, profile_len).astype(jnp.bfloat16)
    pred_ref[...] = dot(picker[...], arrived).astype(jnp.bfloat16)


def fetch(lat_count, lon_count, capacity, cols, background, increment):
    devices = lat_count * lon_count
    column_count, profile_len = background.shape
    slots = cols.shape[1]
    rows = devices * capacity
    return pl.pallas_call(
        functools.partial(fetch_kernel, lat_count, lon_count, capacity),
        out_shape=(
            jax.ShapeDtypeStruct((slots, profile_len), jnp.bfloat16),
            jax.ShapeDtypeStruct((1, slots), jnp.int32),
            jax.ShapeDtypeStruct((1, rows), jnp.int32),
        ),
        in_specs=[VMEM] * 3,
        out_specs=(VMEM,) * 3,
        scratch_shapes=[
            pltpu.VMEM((devices, 1, SPAN), jnp.float32),
            pltpu.VMEM((devices, 1, SPAN), jnp.float32),
            pltpu.VMEM((column_count, profile_len), jnp.bfloat16),
            pltpu.VMEM((devices, capacity, profile_len), jnp.bfloat16),
            pltpu.VMEM((devices, capacity, profile_len), jnp.bfloat16),
            pltpu.VMEM((slots, rows), jnp.bfloat16),
        ]
        + [pltpu.SemaphoreType.DMA((devices,))] * 4,
        compiler_params=pltpu.CompilerParams(
            collective_id=0, has_side_effects=True, vmem_limit_bytes=GRANT
        ),
        name="fetch_profiles",
    )(cols, background, increment)


def compute_kernel(
    block_len,
    scaling,
    count_ref,
    pred_ref,
    side_ref,
    coef_ref,
    dep_ref,
    beta_ref,
    weight_ref,
    rad_ref,
    pulled_ref,
    bias_ref,
    left,
    flip,
    total,
    main,
    rest,
):
    step = pl.program_id(0)
    profile_len = pred_ref.shape[1]
    npredictors, tile = beta_ref.shape

    @pl.when(step == 0)
    def _():
        left[:, :profile_len] = pred_ref[...]
        side = side_ref[...]
        side_main = side.astype(jnp.bfloat16).astype(jnp.float32)
        side_rest = side - side_main
        flip[...] = jnp.concatenate([side_main, side_rest], axis=0).astype(jnp.bfloat16)
        blank = jnp.zeros((SPAN - 3 * npredictors, side.shape[1]), jnp.float32)
        stack = jnp.concatenate([side_main, side_main, side_rest, blank], axis=0)
        left[:, profile_len:] = stack.T.astype(jnp.bfloat16)
        total[...] = jnp.zeros_like(total)

    coef = coef_ref[...]
    beta = beta_ref[...]
    beta_main = beta.astype(jnp.bfloat16).astype(jnp.float32)
    beta_rest = beta - beta_main
    filler = jnp.zeros((SPAN - 3 * npredictors, tile), jnp.float32)
    extra = jnp.concatenate([beta_main, beta_rest, beta_main, filler], axis=0)
    right = jnp.concatenate([coef, extra.astype(jnp.bfloat16)], axis=0)
    weight = weight_ref[...]
    for block in range(pred_ref.shape[0] // block_len):
        part = pl.ds(block * block_len, block_len)
        present = iota((block_len, tile), 0) < count_ref[block]
        radiance = jnp.where(present, dot(left[part, :], right), 0.0)
        rad_ref[part, :] = radiance.astype(jnp.bfloat16)
        misfit = weight * (radiance - dep_ref[part, :].astype(jnp.float32))
        misfit = jnp.where(present, misfit, 0.0)
        misfit_b = misfit.astype(jnp.bfloat16)
        main[part, :] = misfit_b
        rest[part, :] = (misfit - misfit_b.astype(jnp.float32)).astype(jnp.bfloat16)
    total[...] += dot_nt(main[...], coef)
    whole = dot(flip[...], main[...])
    small = dot(flip[...], rest[...])
    share = whole[:npredictors] + whole[npredictors:] + small[:npredictors]
    bias_ref[...] = (scaling * share).astype(bias_ref.dtype)

    @pl.when(step == pl.num_programs(0) - 1)
    def _():
        pulled_ref[...] = total[...].astype(jnp.bfloat16)


def compute(block_len, scaling, obs_count, pred, side, coef, dep, beta, weight):
    slots, profile_len = pred.shape
    channels = coef.shape[1]
    npredictors = side.shape[0]
    tile = max(t for t in range(128, 513, 128) if channels % t == 0)
    def fixed(shape):
        return pl.BlockSpec(shape, lambda i: (0, 0))

    def moving(height):
        return pl.BlockSpec((height, tile), lambda i: (0, i))

    return pl.pallas_call(
        functools.partial(compute_kernel, block_len, scaling),
        grid=(channels // tile,),
        out_shape=(
            jax.ShapeDtypeStruct((slots, channels), jnp.bfloat16),
            jax.ShapeDtypeStruct((slots, profile_len), jnp.bfloat16),
            jax.ShapeDtypeStruct((npredictors, channels), jnp.bfloat16),
        ),
        in_specs=[
            pl.BlockSpec(memory_space=pltpu.SMEM),
            fixed((slots, profile_len)),
            fixed((npredictors, slots)),
            moving(profile_len),
            moving(slots),
            moving(npredictors),
            moving(1),
        ],
        out_specs=(moving(slots), fixed((slots, profile_len)), moving(npredictors)),
        scratch_shapes=[
            pltpu.VMEM((slots, profile_len + SPAN), jnp.bfloat16),
            pltpu.VMEM((2 * npredictors, slots), jnp.bfloat16),
            pltpu.VMEM((slots, profile_len), jnp.float32),
            pltpu.VMEM((slots, tile), jnp.bfloat16),
            pltpu.VMEM((slots, tile), jnp.bfloat16),
        ],
        compiler_params=pltpu.CompilerParams(vmem_limit_bytes=GRANT),
        name="operator",
    )(obs_count, pred, side, coef, dep, beta, weight)


def return_kernel(
    lat_count,
    lon_count,
    capacity,
    pulled_ref,
    position_ref,
    wanted_ref,
    bias_ref,
    base_ref,
    grad_ref,
    sum_ref,
    outbound,
    inbound,
    shares,
    collector,
    jacobian,
    row_send,
    row_recv,
    bias_send,
    bias_recv,
):
    devices = lat_count * lon_count
    column_count, profile_len = base_ref.shape
    slots = pulled_ref.shape[0]
    rows = devices * capacity
    me, peer = peers_of(lat_count, lon_count)
    barrier = greet(devices, peer)
    placed = ones_where(iota((rows, slots), 0) == position_ref[...])
    payload = dot(placed, pulled_ref[...]).reshape(devices, capacity, profile_len)
    outbound[...] = payload.astype(jnp.bfloat16)
    pl.semaphore_wait(barrier, devices - 1)
    send_all(devices, me, peer, outbound, inbound, row_send, row_recv)
    send_all(devices, me, peer, bias_ref, shares, bias_send, bias_recv)
    inbound[me] = outbound[me]
    shares[me] = bias_ref[me]
    collector[...] = ones_where(iota((column_count, rows), 0) == wanted_ref[...])
    jacobian[...] = 1.0 + 0.5 * jnp.tanh(base_ref[...].astype(jnp.float32))
    wait_all(devices, peer, outbound, inbound, row_send, row_recv)
    arrived = inbound[...].astype(jnp.float32).reshape(rows, profile_len).astype(jnp.bfloat16)
    grad_ref[...] = (dot(collector[...], arrived) * jacobian[...]).astype(jnp.bfloat16)
    wait_all(devices, peer, bias_ref, shares, bias_send, bias_recv)
    sum_ref[...] = jnp.sum(shares[...].astype(jnp.float32), axis=0)


def give_back(lat_count, lon_count, capacity, pulled, position, wanted, bias, background):
    devices = lat_count * lon_count
    column_count, profile_len = background.shape
    rows = devices * capacity
    return pl.pallas_call(
        functools.partial(return_kernel, lat_count, lon_count, capacity),
        out_shape=(
            jax.ShapeDtypeStruct(background.shape, jnp.bfloat16),
            jax.ShapeDtypeStruct(bias.shape[1:], jnp.float32),
        ),
        in_specs=[VMEM] * 5,
        out_specs=(VMEM,) * 2,
        scratch_shapes=[
            pltpu.VMEM((devices, capacity, profile_len), jnp.bfloat16),
            pltpu.VMEM((devices, capacity, profile_len), jnp.bfloat16),
            pltpu.VMEM(bias.shape, bias.dtype),
            pltpu.VMEM((column_count, rows), jnp.bfloat16),
            pltpu.VMEM((column_count, profile_len), jnp.float32),
        ]
        + [pltpu.SemaphoreType.DMA((devices,))] * 4,
        compiler_params=pltpu.CompilerParams(
            collective_id=1, has_side_effects=True, vmem_limit_bytes=GRANT
        ),
        name="return_adjoint",
    )(pulled, position, wanted, bias, background)


def shards(
    background,
    increment,
    coefficients,
    departures,
    bias_pred,
    beta_incr,
    obs_weight,
    obs_count,
    col_index,
):
    lat_count = lax.axis_size("lat")
    lon_count = lax.axis_size("lon")
    devices = lat_count * lon_count
    block_count, block_len = col_index.shape
    channels = coefficients.shape[1]
    npredictors = bias_pred.shape[2]
    slot_count = block_count * block_len
    capacity = 8 * pl.cdiv(3 * slot_count // (2 * devices), 8)
    scaling = (slot_count * devices) ** -0.5
    pred, position, wanted = fetch(
        lat_count, lon_count, capacity, col_index.reshape(1, slot_count), background, increment
    )
    radiance, pulled, bias = compute(
        block_len,
        scaling,
        obs_count,
        pred,
        bias_pred.reshape(slot_count, npredictors).T,
        coefficients,
        departures.reshape(slot_count, channels),
        beta_incr,
        obs_weight.reshape(1, channels),
    )
    bias = bias.reshape(npredictors, devices, channels // devices).transpose(1, 0, 2)
    column_grad, bias_grad = give_back(
        lat_count, lon_count, capacity, pulled, position, wanted, bias, background
    )
    return (radiance.reshape(departures.shape), column_grad, bias_grad.T)


def solution(mesh):
    return jax.shard_map(
        shards,
        mesh=mesh,
        in_specs=(
            P(("lat", "lon"), None),
            P(("lat", "lon"), None),
            P(),
            P(("lat", "lon"), None, None),
            P(("lat", "lon"), None, None),
            P(),
            P(),
            P(("lat", "lon")),
            P(("lat", "lon"), None),
        ),
        out_specs=(P(("lat", "lon"), None, None), P(("lat", "lon"), None), P(("lat", "lon"), None)),
        check_vma=False,
    )
```
